32 devices in a mesh: tm: 8 (over z, y), space: 4 (over x, core).
Axes of the slice: x: 2, y: 2, z: 4, core: 2. Of those that a mesh axis runs over, the one named last changes fastest.
Arguments:
- controls: bfloat16 [32, 64, 2048], P('tm', None, 'space'), may hold values from -4 to 4
- target: bfloat16 [64, 2048], P(None, 'space'), may hold values from -4 to 4
- state_in: float32 [8, 64, 2048], P('tm', None, 'space'), may hold values from -2.5 to 2.5
- adjoint_in: float32 [8, 64, 2048], P('tm', None, 'space'), may hold values from -5 to 5
- block_inverse: bfloat16 [64, 64, 2048], P(None, None, 'space'), may hold values from -1 to 1
- numbering: int32 [4, 512], P('space'), may hold values from 0 to 511, each once within a row
Outputs:
- new_controls: bfloat16 [32, 64, 2048], P('tm', None, 'space')
- next_state: float32 [8, 64, 2048], P('tm', None, 'space')
- next_adjoint: float32 [8, 64, 2048], P('tm', None, 'space')
- objective: float32 [], replicated
The draws below stay inside these ranges and needn't reach their ends.
Inputs may be any that keep to these rules, and one draw needn't show every extreme that they name: `numbering`: each row names every structural element of its slab exactly once.
All inputs are finite; a program needn't handle non-finite values.
Results may differ from the reference program's by a relative error of at most 0.0085.
Values may be sent and summed in bfloat16 or wider, within the bound.
A program may use at most 128 MiB of HBM per device.

```python
import math
import jax
import jax.numpy as jnp
from jax import lax

NSIDE = 4
NODES = 64
EXY = 16
ELAYERS = 2
STEP_DEV = 4
E_DEV = 512
ELEMENTS = 2048
SLABS = 4
TSLICES = 8
STEPS = 32


def draw_block_inverse(key, part):
    first_key, second_key = jax.random.split(key)
    dims = (NODES, NODES, ELEMENTS)
    spread = jax.random.truncated_normal(first_key, -4.0, 4.0, dims, jnp.float32) * (0.15 / NODES ** 0.5)
    diagonal = jnp.exp(jax.random.uniform(second_key, (NODES, ELEMENTS), jnp.float32, math.log(0.55), 0.0))
    row_index = lax.broadcasted_iota(jnp.int32, (NODES, NODES), 0)
    column_index = lax.broadcasted_iota(jnp.int32, (NODES, NODES), 1)
    unit_mask = (row_index == column_index).astype(jnp.float32)[:, :, None]
    return (spread * (1.0 - unit_mask) + unit_mask * diagonal[None, :, :]).astype(jnp.bfloat16)


def block_scale(stream_key, extent, pieces, smallest, top_value):
    level, own = 1.0, jax.random.fold_in(stream_key, 6)
    for dim, shards_of in pieces:
        heights = jnp.exp(jax.random.uniform(jax.random.fold_in(own, dim), (shards_of,), jnp.float32, smallest / len(pieces), top_value / len(pieces)))
        level = level * jnp.repeat(heights, extent[dim] // shards_of).reshape([-1 if axis == dim else 1 for axis in range(len(extent))])
    return level


def normal_values(own_key, extent, deviation, bound, cuts=(), held_as=jnp.bfloat16):
    level = block_scale(own_key, extent, cuts, -0.22, 0.18) if cuts else 1.0
    values = jax.random.normal(own_key, extent, jnp.float32) * deviation * level
    return jnp.minimum(jnp.maximum(values, -bound), bound).astype(held_as)


def setup_inputs(seed: int = 0) -> dict:
    splits = jax.random.split(jax.random.key(seed), 7)
    controls = normal_values(splits[0], (STEPS, NODES, ELEMENTS), 1.0, 4.0, ((0, 8), (2, 4)))
    target = normal_values(splits[1], (NODES, ELEMENTS), 1.0, 4.0, ((1, 4),))
    state_in = normal_values(splits[2], (TSLICES, NODES, ELEMENTS), 0.5, 2.5, ((0, 8), (2, 4)), jnp.float32)
    adjoint_in = normal_values(splits[3], (TSLICES, NODES, ELEMENTS), 1.0, 5.0, ((0, 8), (2, 4)), jnp.float32)
    block_inverse = draw_block_inverse(jax.random.fold_in(splits[6], 71), 0)
    numbering = jax.vmap(lambda own: jax.random.permutation(own, E_DEV))(jax.random.split(splits[5], SLABS)).reshape((SLABS, E_DEV)).astype(jnp.int32)
    return {"controls": controls, "target": target, "state_in": state_in, "adjoint_in": adjoint_in, "block_inverse": block_inverse, "numbering": numbering}


TIME_STEP = 0.1
PENALTY = 0.5
REGULAR = 0.1


def shift_layers(traces, upward):
    empty = jnp.zeros_like(traces[:, :, :, :1])
    if upward:
        return jnp.concatenate([empty, traces[:, :, :, :-1]], axis=3)
    return jnp.concatenate([traces[:, :, :, 1:], empty], axis=3)


def face_jumps(values, node_side, layers_all, width):
    leading = values.shape[0]
    tensor = values.reshape(leading, node_side, node_side, node_side, layers_all, width, width)
    last = node_side - 1
    west = jnp.roll(tensor[:, :, :, last], 1, axis=-1) - tensor[:, :, :, 0]
    east = jnp.roll(tensor[:, :, :, 0], -1, axis=-1) - tensor[:, :, :, last]
    south = jnp.roll(tensor[:, :, last], 1, axis=-2) - tensor[:, :, 0]
    north = jnp.roll(tensor[:, :, 0], -1, axis=-2) - tensor[:, :, last]
    lower = shift_layers(tensor[:, last], True) - tensor[:, 0]
    upper = shift_layers(tensor[:, 0], False) - tensor[:, last]
    total = jnp.zeros_like(tensor)
    total = total.at[:, :, :, 0].add(west)
    total = total.at[:, :, :, last].add(east)
    total = total.at[:, :, 0].add(south)
    total = total.at[:, :, last].add(north)
    total = total.at[:, 0].add(lower)
    total = total.at[:, last].add(upper)
    return total.reshape(values.shape)


def reference(controls, target, state_in, adjoint_in, block_inverse, numbering):
    slabs, per_slab = numbering.shape
    rows = jnp.broadcast_to(jnp.arange(slabs, dtype=jnp.int32)[:, None], (slabs, per_slab))
    columns = jnp.broadcast_to(jnp.arange(per_slab, dtype=jnp.int32)[None, :], (slabs, per_slab))
    inverse = jnp.zeros((slabs, per_slab), jnp.int32).at[rows, numbering].set(columns)
    to_struct = (rows * per_slab + inverse).reshape(-1).astype(jnp.int32)
    to_store = (rows * per_slab + numbering).reshape(-1).astype(jnp.int32)
    layers_all = slabs * ELAYERS
    slices = state_in.shape[0]
    blocks = jnp.take(block_inverse, to_struct, axis=-1).astype(jnp.float32)
    goal = jnp.take(target, to_struct, axis=-1).astype(jnp.float32)
    control_all = jnp.take(controls, to_struct, axis=-1).astype(jnp.float32)
    control_all = control_all.reshape(slices, STEP_DEV, NODES, ELEMENTS)
    state = jnp.take(state_in, to_struct, axis=-1)
    start_adjoint = jnp.take(adjoint_in, to_struct, axis=-1)
    first_steps = (jnp.arange(slices, dtype=jnp.int32) * STEP_DEV).astype(jnp.float32)[:, None, None]

    def jumps(values):
        return face_jumps(values, NSIDE, layers_all, EXY)

    def forward_apply(right_side):
        return jnp.einsum("ije,tje->tie", blocks, right_side.astype(jnp.float32), precision=lax.Precision.HIGHEST)

    def backward_apply(vector):
        return jnp.einsum("ije,tie->tje", blocks, vector.astype(jnp.float32), precision=lax.Precision.HIGHEST)

    history = [state]
    misfit = jnp.float32(0.0)
    for index_k in range(STEP_DEV):
        control_now = control_all[:, index_k]
        right_side = (state + TIME_STEP * (state - state * state * state) + TIME_STEP * PENALTY * jumps(state)
                      + TIME_STEP * control_now).astype(jnp.bfloat16)
        state = forward_apply(right_side)
        history.append(state)
        weight = (first_steps + (index_k + 1)) / STEPS
        misfit = misfit + jnp.sum(weight * (state - goal) ** 2)
    regular_sum = jnp.sum(control_all * control_all)
    objective = (0.5 * misfit + 0.5 * REGULAR * regular_sum) / (STEPS * NODES * ELEMENTS)

    adjoint = (first_steps + STEP_DEV) / STEPS * (history[-1] - goal) + start_adjoint
    updated = [None] * STEP_DEV
    carried = adjoint
    for index_k in reversed(range(STEP_DEV)):
        pulled = backward_apply(adjoint.astype(jnp.bfloat16))
        control_now = control_all[:, index_k]
        updated[index_k] = (control_now - (TIME_STEP * pulled + REGULAR * control_now)).astype(jnp.bfloat16)
        before = history[index_k]
        carried = pulled + TIME_STEP * (1.0 - 3.0 * before * before) * pulled + TIME_STEP * PENALTY * jumps(pulled)
        if index_k > 0:
            weight = (first_steps + index_k) / STEPS
            adjoint = weight * (before - goal) + carried
    new_controls = jnp.stack(updated, axis=1).reshape(STEPS, NODES, ELEMENTS)
    new_controls = jnp.take(new_controls, to_store, axis=-1)
    next_state = jnp.concatenate([history[0][:1], history[-1][:-1]], axis=0)
    next_state = jnp.take(next_state, to_store, axis=-1)
    next_adjoint = jnp.concatenate([carried[1:], jnp.zeros_like(carried[:1])], axis=0)
    next_adjoint = jnp.take(next_adjoint, to_store, axis=-1)
    return new_controls, next_state, next_adjoint, objective
```

```python
import functools

import jax
import jax.numpy as jnp
from jax import lax
from jax.experimental import pallas as pl
from jax.experimental.pallas import tpu as pltpu
from jax.sharding import PartitionSpec as P

NSIDE = 4
EXY = 16
BLOCK = NSIDE * NSIDE
HALF = 2 * BLOCK
LAYER = EXY * EXY
TIME_STEP = 0.1
PENALTY = 0.5
REGULAR = 0.1
F32 = jnp.float32
BF16 = jnp.bfloat16
RIM, MID = 0, 1
WIDE = 256


def dot(a, b):
    return jnp.dot(a, b, preferred_element_type=F32)


def rows_of(half):
    if half == RIM:
        return ((0, BLOCK), (3 * BLOCK, BLOCK))
    return ((BLOCK, BLOCK), (2 * BLOCK, BLOCK))


def take(ref, half, *lead):
    return jnp.concatenate([ref[lead + (slice(s, s + n),)] for s, n in rows_of(half)], axis=0)


def put(ref, half, value, *lead):
    at = 0
    for s, n in rows_of(half):
        ref[lead + (slice(s, s + n),)] = value[at : at + n]
        at += n


def fold(x):
    total = None
    for i in range(0, x.shape[0], 8):
        for j in range(0, x.shape[1], 128):
            piece = x[i : i + 8, j : j + 128]
            total = piece if total is None else total + piece
    return total


def lateral(x):
    rows, lanes = x.shape
    q = lax.broadcasted_iota(jnp.int32, x.shape, 0)
    s = lax.broadcasted_iota(jnp.int32, x.shape, 1)
    a, b = q % NSIDE, (q // NSIDE) % NSIDE
    col, row = s % EXY, (s // EXY) % EXY
    last = NSIDE - 1

    def along(which, node_step, place, lane_step):
        back = (EXY - 1) * lane_step
        low = which == 0
        z = jnp.where(low, pltpu.roll(x, rows - last * node_step, 0), pltpu.roll(x, last * node_step, 0))
        down = jnp.where(place == 0, pltpu.roll(z, lanes - back, 1), pltpu.roll(z, lane_step, 1))
        up = jnp.where(place == EXY - 1, pltpu.roll(z, back, 1), pltpu.roll(z, lanes - lane_step, 1))
        return jnp.where(low, down, jnp.where(which == last, up, 0.0))

    return along(a, 1, col, 1) + along(b, NSIDE, row, EXY)


def faces(half, shape):
    q = lax.broadcasted_iota(jnp.int32, shape, 0)
    a, b = q % NSIDE, (q // NSIDE) % NSIDE
    last = NSIDE - 1
    count = jnp.where((a == 0) | (a == last), 1.0, 0.0) + jnp.where((b == 0) | (b == last), 1.0, 0.0)
    return count + (1.0 if half == RIM else 0.0)


def kernel(
    n_space, n_tm,
    num_ref, ctl_hbm, tgt_hbm, st_hbm, adj_hbm, a_hbm,
    newc_ref, nst_ref, nadj_ref, obj_ref,
    a_ref, ctl, tgt, adj, st, hist, goal, r_ref, gf, pulled, part, xr, pa, pt,
    cost, rim_out, rim_in, st_out, st_in, adj_out, adj_in, slot_s, slot_t,
    in_sem, a_sem, rim_send, rim_recv, st_sem, adj_send_sem, adj_recv_sem,
    ss_send, ss_recv, tt_send, tt_recv,
):
    steps = ctl.shape[0]
    elements = ctl.shape[2]
    nodes = ctl.shape[1]
    me = lax.axis_index("space")
    t = lax.axis_index("tm")
    first = t * steps
    total_steps = steps * n_tm

    def weight(k):
        return (first + k).astype(F32) / total_steps

    loads = [
        pltpu.make_async_copy(src, dst, in_sem.at[i])
        for i, (src, dst) in enumerate(
            ((st_hbm.at[0], st), (ctl_hbm, ctl), (tgt_hbm, tgt), (adj_hbm.at[0], adj))
        )
    ]
    for c in loads:
        c.start()
    parts = a_sem.shape[0]
    chunk = nodes // parts
    a_loads = [
        pltpu.make_async_copy(a_hbm.at[pl.ds(i * chunk, chunk)], a_ref.at[pl.ds(i * chunk, chunk)], a_sem.at[i])
        for i in range(parts)
    ]
    for c in a_loads:
        c.start()

    rim_in[...] = jnp.zeros_like(rim_in)
    barrier = pltpu.get_barrier_semaphore()
    for d in range(1, n_space):
        pl.semaphore_signal(barrier, inc=1, device_id={"space": lax.rem(me + d, n_space)},
                            device_id_type=pl.DeviceIdType.MESH)
    for d in range(1, n_tm):
        pl.semaphore_signal(barrier, inc=1, device_id={"tm": lax.rem(t + d, n_tm)},
                            device_id_type=pl.DeviceIdType.MESH)

    for i in range(0, elements, WIDE):
        place = lax.broadcasted_iota(jnp.int32, (WIDE, elements), 0) + i
        hot = jnp.where(num_ref[...] == place, 1.0, 0.0)
        pt[i : i + WIDE, :] = hot.astype(BF16)
        pa[:, i : i + WIDE] = hot.T.astype(BF16)

    cost[...] = jnp.zeros_like(cost)

    def arrange(x):
        return dot(x.astype(BF16), pa[...])

    def restore(x):
        return dot(x.astype(BF16), pt[...])

    def rim_copy(rnd, side):
        peer = me - 1 if side == 0 else me + 1
        return pltpu.make_async_remote_copy(
            src_ref=rim_out.at[rnd, side], dst_ref=rim_in.at[rnd, 1 - side],
            send_sem=rim_send.at[rnd, side], recv_sem=rim_recv.at[rnd, 1 - side],
            device_id={"space": peer}, device_id_type=pl.DeviceIdType.MESH,
        )

    def send_rims(rnd, x):
        rim_out[rnd, 0] = x[:BLOCK, :LAYER].astype(BF16)
        rim_out[rnd, 1] = x[BLOCK:, elements - LAYER :].astype(BF16)

        @pl.when(me > 0)
        def _():
            rim_copy(rnd, 0).start()

        @pl.when(me < n_space - 1)
        def _():
            rim_copy(rnd, 1).start()

    def arrival(rnd, side):
        peer = me - 1 if side == 0 else me + 1
        return pltpu.make_async_remote_copy(
            src_ref=rim_out.at[rnd, side], dst_ref=rim_in.at[rnd, side],
            send_sem=rim_send.at[rnd, side], recv_sem=rim_recv.at[rnd, side],
            device_id={"space": peer}, device_id_type=pl.DeviceIdType.MESH,
        )

    def wait_rims(rnd):
        @pl.when(me > 0)
        def _():
            arrival(rnd, 0).wait()

        @pl.when(me < n_space - 1)
        def _():
            arrival(rnd, 1).wait()

    def rim_neighbours(rnd, x, lat):
        below = jnp.concatenate([rim_in[rnd, 0].astype(F32), x[BLOCK:, : elements - LAYER]], axis=1)
        above = jnp.concatenate([x[:BLOCK, LAYER:], rim_in[rnd, 1].astype(F32)], axis=1)
        return restore(lat + jnp.concatenate([below, above], axis=0))

    group = 8
    depth = group * HALF
    k_f = lax.broadcasted_iota(jnp.int32, (group, depth), 1) // HALF
    sum_rows = jnp.where(k_f == lax.broadcasted_iota(jnp.int32, (group, depth), 0), 1.0, 0.0).astype(BF16)
    k_b = lax.broadcasted_iota(jnp.int32, (HALF, depth), 1) % HALF
    sum_groups = jnp.where(k_b == lax.broadcasted_iota(jnp.int32, (HALF, depth), 0), 1.0, 0.0).astype(BF16)

    def groups_of(half):
        return [s + i for s, n in rows_of(half) for i in range(0, n, group)]

    def block_rows(i0, in_half, lanes):
        return jnp.concatenate(
            [a_ref[i0 : i0 + group, s : s + n, lanes] for s, n in rows_of(in_half)], axis=1
        )

    def apply(out_half, in_half, write):
        for n0 in range(0, elements, WIDE):
            lanes = slice(n0, n0 + WIDE)
            right = r_ref[in_half, :, lanes]
            for at, i0 in enumerate(groups_of(out_half)):
                q = (block_rows(i0, in_half, lanes) * right[None]).reshape(depth, WIDE)
                write(slice(at * group, (at + 1) * group), lanes, dot(sum_rows, q))

    def apply_t(out_half, in_half, write):
        for n0 in range(0, elements, WIDE):
            lanes = slice(n0, n0 + WIDE)
            acc = None
            for at, i0 in enumerate(groups_of(in_half)):
                pieces = []
                for i in range(group):
                    row = gf[in_half, at * group + i : at * group + i + 1, lanes]
                    spread = jnp.broadcast_to(row, (BLOCK, WIDE)).astype(BF16)
                    for s, n in rows_of(out_half):
                        pieces.append(a_ref[i0 + i, s : s + n, lanes] * spread)
                now = dot(sum_groups, jnp.concatenate(pieces, axis=0))
                acc = now if acc is None else acc + now
            write(lanes, acc)

    shape = (HALF, elements)

    def rhs(half, u, n, control):
        return (
            u + TIME_STEP * (u - u * u * u)
            + TIME_STEP * PENALTY * (n - faces(half, shape) * u)
            + TIME_STEP * control
        ).astype(BF16)

    loads[0].wait()
    for half in (RIM, MID):
        hist[0, half] = take(st, half)
    x0 = arrange(hist[0, RIM])
    xr[...] = x0
    pl.semaphore_wait(barrier, n_space - 1 + n_tm - 1)
    send_rims(0, x0)
    for c in loads[1:]:
        c.wait()
    for half in (RIM, MID):
        goal[half] = take(tgt, half).astype(F32)

    def forward(k, carry):
        um = hist[k, MID]
        nm = restore(lateral(arrange(um)))
        cm = take(ctl, MID, k).astype(F32)
        cr = take(ctl, RIM, k).astype(F32)
        r_ref[MID] = rhs(MID, um, nm, cm)
        x = xr[...]
        lat = lateral(x)

        @pl.when(k == 0)
        def _():
            for c in a_loads:
                c.wait()

        for out in (RIM, MID):
            def write(rows, lanes, v, out=out):
                hist[k + 1, out, rows, lanes] = v
            apply(out, MID, write)
        ur = hist[k, RIM]
        w = jnp.where(k > 0, weight(k), 0.0)
        dm, dr = um - goal[MID], ur - goal[RIM]
        cost[...] += 0.5 * w * fold(dm * dm + dr * dr) + 0.5 * REGULAR * fold(cm * cm + cr * cr)

        wait_rims(k)
        nr = rim_neighbours(k, x, lat)
        r_ref[RIM] = rhs(RIM, ur, nr, cr)

        def add(out):
            def write(rows, lanes, v):
                hist[k + 1, out, rows, lanes] += v
            return write

        apply(RIM, RIM, add(RIM))

        @pl.when(k < steps - 1)
        def _():
            y = arrange(hist[k + 1, RIM])
            xr[...] = y
            send_rims(k + 1, y)

        apply(MID, RIM, add(MID))
        return carry

    lax.fori_loop(0, steps, forward, 0)

    w_end = weight(steps)
    for half in (MID, RIM):
        u = hist[steps, half]
        d = u - goal[half]
        cost[...] += 0.5 * w_end * fold(d * d)
        gf[half] = w_end * d + take(adj, half)
        st_out[half] = u.astype(BF16)

    def st_copy(dst):
        return pltpu.make_async_remote_copy(
            src_ref=st_out, dst_ref=st_in, send_sem=st_sem.at[0], recv_sem=st_sem.at[1],
            device_id={"tm": dst}, device_id_type=pl.DeviceIdType.MESH)

    @pl.when(t < n_tm - 1)
    def _():
        st_copy(t + 1).start()

    slot_s[me] = cost[...]

    def gather_copy(slots, send, recv, axis, index, count, d):
        return pltpu.make_async_remote_copy(
            src_ref=slots.at[index], dst_ref=slots.at[index], send_sem=send.at[d], recv_sem=recv.at[index],
            device_id={axis: lax.rem(index + d, count)}, device_id_type=pl.DeviceIdType.MESH)

    def gather_wait(slots, send, recv, axis, index, count, d):
        gather_copy(slots, send, recv, axis, index, count, d).wait_send()
        origin = lax.rem(index + d, count)
        pltpu.make_async_remote_copy(
            src_ref=slots.at[origin], dst_ref=slots.at[origin], send_sem=send.at[d], recv_sem=recv.at[origin],
            device_id={axis: origin}, device_id_type=pl.DeviceIdType.MESH).wait_recv()

    over_s = (slot_s, ss_send, ss_recv, "space", me, n_space)
    over_t = (slot_t, tt_send, tt_recv, "tm", t, n_tm)
    for d in range(1, n_space):
        gather_copy(*over_s, d).start()

    def part_write(out):
        def write(lanes, v):
            part[out, :, lanes] = v
        return write

    def pulled_write(out):
        def write(lanes, v):
            pulled[out, :, lanes] = part[out, :, lanes] + v
        return write

    def finish(rnd):
        apply_t(RIM, RIM, pulled_write(RIM))
        y = arrange(pulled[RIM])
        xr[...] = y
        send_rims(rnd, y)
        apply_t(MID, RIM, pulled_write(MID))

    def carry_back(half, k, p, n):
        before = hist[k, half]
        carried = (
            p + TIME_STEP * (1.0 - 3.0 * before * before) * p
            + TIME_STEP * PENALTY * (n - faces(half, shape) * p)
        )
        return before, carried

    def update(half, k, p):
        control = take(ctl, half, k).astype(F32)
        put(newc_ref, half, (control - (TIME_STEP * p + REGULAR * control)).astype(BF16), k)

    apply_t(RIM, MID, part_write(RIM))
    apply_t(MID, MID, part_write(MID))
    finish(steps)

    def backward(i, carry):
        k = steps - 1 - i
        rnd = steps + i
        pm = pulled[MID]
        nm = restore(lateral(arrange(pm)))
        before, carried = carry_back(MID, k, pm, nm)
        gf[MID] = weight(k) * (before - goal[MID]) + carried
        x = xr[...]
        lat = lateral(x)
        apply_t(RIM, MID, part_write(RIM))
        apply_t(MID, MID, part_write(MID))
        pr = pulled[RIM]
        update(MID, k, pm)
        update(RIM, k, pr)

        @pl.when(i == 1)
        def _():
            for d in range(1, n_space):
                gather_wait(*over_s, d)
            total = slot_s[0]
            for j in range(1, n_space):
                total = total + slot_s[j]
            slot_t[t] = total
            for d in range(1, n_tm):
                gather_copy(*over_t, d).start()

        wait_rims(rnd)
        nr = rim_neighbours(rnd, x, lat)
        before_r, carried_r = carry_back(RIM, k, pr, nr)
        gf[RIM] = weight(k) * (before_r - goal[RIM]) + carried_r
        finish(rnd + 1)
        return carry

    lax.fori_loop(0, steps - 1, backward, 0)

    def adj_copy(dst, half):
        return pltpu.make_async_remote_copy(
            src_ref=adj_out.at[half], dst_ref=adj_in.at[half], send_sem=adj_send_sem.at[half],
            recv_sem=adj_recv_sem.at[half], device_id={"tm": dst}, device_id_type=pl.DeviceIdType.MESH)

    def send_adj(half, carried):
        adj_out[half] = carried.astype(adj_out.dtype)

        @pl.when(t > 0)
        def _():
            adj_copy(t - 1, half).start()

    rnd = 2 * steps - 1
    pm, pr = pulled[MID], pulled[RIM]
    nm = restore(lateral(arrange(pm)))
    send_adj(MID, carry_back(MID, 0, pm, nm)[1])
    x = xr[...]
    lat = lateral(x)
    wait_rims(rnd)
    nr = rim_neighbours(rnd, x, lat)
    send_adj(RIM, carry_back(RIM, 0, pr, nr)[1])
    update(MID, 0, pm)
    update(RIM, 0, pr)

    @pl.when(t == 0)
    def _():
        nst_ref[0] = st[...]

    @pl.when(t > 0)
    def _():
        st_copy(t - 1).wait_recv()
        for half in (RIM, MID):
            put(nst_ref, half, st_in[half].astype(F32), 0)

    @pl.when(t < n_tm - 1)
    def _():
        st_copy(t + 1).wait_send()

    for d in range(1, n_tm):
        gather_wait(*over_t, d)
    total = slot_t[0]
    for j in range(1, n_tm):
        total = total + slot_t[j]
    obj_ref[0, 0] = jnp.sum(total) * (1.0 / (total_steps * nodes * elements * n_space))

    @pl.when(t == n_tm - 1)
    def _():
        nadj_ref[...] = jnp.zeros_like(nadj_ref)

    @pl.when(t < n_tm - 1)
    def _():
        for half in (MID, RIM):
            adj_copy(t + 1, half).wait_recv()
            put(nadj_ref, half, adj_in[half].astype(F32), 0)

    @pl.when(t > 0)
    def _():
        for half in (MID, RIM):
            adj_copy(t - 1, half).wait_send()


def solution(mesh):
    n_space, n_tm = mesh.shape["space"], mesh.shape["tm"]

    def per_device(controls, target, state_in, adjoint_in, block_inverse, numbering):
        steps, nodes, elements = controls.shape
        vm = pl.BlockSpec(memory_space=pltpu.VMEM)
        anyspace = pl.BlockSpec(memory_space=pl.ANY)
        halves = (2, HALF, elements)
        rounds = 2 * steps
        dma = pltpu.SemaphoreType.DMA
        new_controls, next_state, next_adjoint, objective = pl.pallas_call(
            functools.partial(kernel, n_space, n_tm),
            out_shape=(
                jax.ShapeDtypeStruct(controls.shape, BF16),
                jax.ShapeDtypeStruct(state_in.shape, F32),
                jax.ShapeDtypeStruct(adjoint_in.shape, F32),
                jax.ShapeDtypeStruct((1, 1), F32),
            ),
            in_specs=[vm, anyspace, anyspace, anyspace, anyspace, anyspace],
            out_specs=(vm, vm, vm, pl.BlockSpec(memory_space=pltpu.SMEM)),
            scratch_shapes=[
                pltpu.VMEM(block_inverse.shape, BF16),
                pltpu.VMEM(controls.shape, BF16),
                pltpu.VMEM(target.shape, BF16),
                pltpu.VMEM(adjoint_in.shape[1:], F32),
                pltpu.VMEM(state_in.shape[1:], F32),
                pltpu.VMEM((steps + 1,) + halves, F32),
                pltpu.VMEM(halves, F32),
                pltpu.VMEM(halves, BF16),
                pltpu.VMEM(halves, F32),
                pltpu.VMEM(halves, F32),
                pltpu.VMEM(halves, F32),
                pltpu.VMEM(halves[1:], F32),
                pltpu.VMEM((elements, elements), BF16),
                pltpu.VMEM((elements, elements), BF16),
                pltpu.VMEM((8, 128), F32),
                pltpu.VMEM((rounds, 2, BLOCK, LAYER), BF16),
                pltpu.VMEM((rounds, 2, BLOCK, LAYER), BF16),
                pltpu.VMEM(halves, BF16),
                pltpu.VMEM(halves, BF16),
                pltpu.VMEM(halves, BF16),
                pltpu.VMEM(halves, BF16),
                pltpu.VMEM((n_space, 8, 128), F32),
                pltpu.VMEM((n_tm, 8, 128), F32),
                dma((4,)),
                dma((4,)),
                dma((rounds, 2)),
                dma((rounds, 2)),
                dma((2,)),
                dma((2,)),
                dma((2,)),
                dma((n_space,)),
                dma((n_space,)),
                dma((n_tm,)),
                dma((n_tm,)),
            ],
            compiler_params=pltpu.CompilerParams(
                collective_id=0, has_side_effects=True, vmem_limit_bytes=67043328
            ),
        )(numbering, controls, target, state_in, adjoint_in, block_inverse)
        return new_controls, next_state, next_adjoint, objective.reshape(())

    return jax.shard_map(
        per_device,
        mesh=mesh,
        in_specs=(
            P("tm", None, "space"),
            P(None, "space"),
            P("tm", None, "space"),
            P("tm", None, "space"),
            P(None, None, "space"),
            P("space", None),
        ),
        out_specs=(P("tm", None, "space"), P("tm", None, "space"), P("tm", None, "space"), P()),
        check_vma=False,
    )
```

```python
import functools

import jax
import jax.numpy as jnp
from jax import lax
from jax.experimental import pallas as pl
from jax.experimental.pallas import tpu as pltpu
from jax.sharding import PartitionSpec as P

NSIDE = 4
EXY = 16
BLOCK = NSIDE * NSIDE
HALF = 2 * BLOCK
LAYER = EXY * EXY
TIME_STEP = 0.1
PENALTY = 0.5
REGULAR = 0.1
F32 = jnp.float32
BF16 = jnp.bfloat16
RIM, MID = 0, 1
WIDE = 256


def dot(a, b):
    return jnp.dot(a, b, preferred_element_type=F32)


def rows_of(half):
    if half == RIM:
        return ((0, BLOCK), (3 * BLOCK, BLOCK))
    return ((BLOCK, BLOCK), (2 * BLOCK, BLOCK))


def take(ref, half, *lead):
    return jnp.concatenate([ref[lead + (slice(s, s + n),)] for s, n in rows_of(half)], axis=0)


def put(ref, half, value, *lead):
    at = 0
    for s, n in rows_of(half):
        ref[lead + (slice(s, s + n),)] = value[at : at + n]
        at += n


def fold(x):
    total = None
    for i in range(0, x.shape[0], 8):
        for j in range(0, x.shape[1], 128):
            piece = x[i : i + 8, j : j + 128]
            total = piece if total is None else total + piece
    return total


def lateral(x):
    rows, lanes = x.shape
    q = lax.broadcasted_iota(jnp.int32, x.shape, 0)
    s = lax.broadcasted_iota(jnp.int32, x.shape, 1)
    a, b = q % NSIDE, (q // NSIDE) % NSIDE
    col, row = s % EXY, (s // EXY) % EXY
    last = NSIDE - 1

    def along(which, node_step, place, lane_step):
        back = (EXY - 1) * lane_step
        low = which == 0
        z = jnp.where(low, pltpu.roll(x, rows - last * node_step, 0), pltpu.roll(x, last * node_step, 0))
        down = jnp.where(place == 0, pltpu.roll(z, lanes - back, 1), pltpu.roll(z, lane_step, 1))
        up = jnp.where(place == EXY - 1, pltpu.roll(z, back, 1), pltpu.roll(z, lanes - lane_step, 1))
        return jnp.where(low, down, jnp.where(which == last, up, 0.0))

    return along(a, 1, col, 1) + along(b, NSIDE, row, EXY)


def faces(half, shape):
    q = lax.broadcasted_iota(jnp.int32, shape, 0)
    a, b = q % NSIDE, (q // NSIDE) % NSIDE
    last = NSIDE - 1
    count = jnp.where((a == 0) | (a == last), 1.0, 0.0) + jnp.where((b == 0) | (b == last), 1.0, 0.0)
    return count + (1.0 if half == RIM else 0.0)


def kernel(
    n_space, n_tm,
    num_ref, ctl_hbm, tgt_hbm, st_hbm, adj_hbm, a_hbm,
    newc_ref, nst_ref, nadj_ref, obj_ref,
    a_ref, ctl, tgt, adj, st, hist, goal, r_ref, gf, pulled, part, xr, pa, pt,
    cost, rim_out, rim_in, st_out, st_in, adj_out, adj_in, slot_s, slot_t,
    in_sem, a_sem, rim_send, rim_recv, st_sem, adj_send_sem, adj_recv_sem,
    ss_send, ss_recv, tt_send, tt_recv,
):
    steps = ctl.shape[0]
    elements = ctl.shape[2]
    nodes = ctl.shape[1]
    me = lax.axis_index("space")
    t = lax.axis_index("tm")
    first = t * steps
    total_steps = steps * n_tm

    def weight(k):
        return (first + k).astype(F32) / total_steps

    loads = [
        pltpu.make_async_copy(src, dst, in_sem.at[i])
        for i, (src, dst) in enumerate(
            ((st_hbm.at[0], st), (ctl_hbm, ctl), (tgt_hbm, tgt), (adj_hbm.at[0], adj))
        )
    ]
    for c in loads:
        c.start()
    parts = a_sem.shape[0]
    chunk = nodes // parts
    a_loads = [
        pltpu.make_async_copy(a_hbm.at[pl.ds(i * chunk, chunk)], a_ref.at[pl.ds(i * chunk, chunk)], a_sem.at[i])
        for i in range(parts)
    ]
    for c in a_loads:
        c.start()

    rim_in[...] = jnp.zeros_like(rim_in)
    barrier = pltpu.get_barrier_semaphore()
    for d in range(1, n_space):
        pl.semaphore_signal(barrier, inc=1, device_id={"space": lax.rem(me + d, n_space)},
                            device_id_type=pl.DeviceIdType.MESH)
    for d in range(1, n_tm):
        pl.semaphore_signal(barrier, inc=1, device_id={"tm": lax.rem(t + d, n_tm)},
                            device_id_type=pl.DeviceIdType.MESH)

    for i in range(0, elements, WIDE):
        place = lax.broadcasted_iota(jnp.int32, (WIDE, elements), 0) + i
        hot = jnp.where(num_ref[...] == place, 1.0, 0.0)
        pt[i : i + WIDE, :] = hot.astype(BF16)
        pa[:, i : i + WIDE] = hot.T.astype(BF16)

    cost[...] = jnp.zeros_like(cost)

    def arrange(x):
        return dot(x.astype(BF16), pa[...])

    def restore(x):
        return dot(x.astype(BF16), pt[...])

    def rim_copy(rnd, side):
        peer = me - 1 if side == 0 else me + 1
        return pltpu.make_async_remote_copy(
            src_ref=rim_out.at[rnd, side], dst_ref=rim_in.at[rnd, 1 - side],
            send_sem=rim_send.at[rnd, side], recv_sem=rim_recv.at[rnd, 1 - side],
            device_id={"space": peer}, device_id_type=pl.DeviceIdType.MESH,
        )

    def send_rims(rnd, x):
        rim_out[rnd, 0] = x[:BLOCK, :LAYER].astype(BF16)
        rim_out[rnd, 1] = x[BLOCK:, elements - LAYER :].astype(BF16)

        @pl.when(me > 0)
        def _():
            rim_copy(rnd, 0).start()

        @pl.when(me < n_space - 1)
        def _():
            rim_copy(rnd, 1).start()

    def arrival(rnd, side):
        peer = me - 1 if side == 0 else me + 1
        return pltpu.make_async_remote_copy(
            src_ref=rim_out.at[rnd, side], dst_ref=rim_in.at[rnd, side],
            send_sem=rim_send.at[rnd, side], recv_sem=rim_recv.at[rnd, side],
            device_id={"space": peer}, device_id_type=pl.DeviceIdType.MESH,
        )

    def wait_rims(rnd):
        @pl.when(me > 0)
        def _():
            arrival(rnd, 0).wait()

        @pl.when(me < n_space - 1)
        def _():
            arrival(rnd, 1).wait()

    def rim_neighbours(rnd, x, lat):
        below = jnp.concatenate([rim_in[rnd, 0].astype(F32), x[BLOCK:, : elements - LAYER]], axis=1)
        above = jnp.concatenate([x[:BLOCK, LAYER:], rim_in[rnd, 1].astype(F32)], axis=1)
        return restore(lat + jnp.concatenate([below, above], axis=0))

    group = 8
    depth = group * HALF
    k_f = lax.broadcasted_iota(jnp.int32, (group, depth), 1) // HALF
    sum_rows = jnp.where(k_f == lax.broadcasted_iota(jnp.int32, (group, depth), 0), 1.0, 0.0).astype(BF16)
    k_b = lax.broadcasted_iota(jnp.int32, (HALF, depth), 1) % HALF
    sum_groups = jnp.where(k_b == lax.broadcasted_iota(jnp.int32, (HALF, depth), 0), 1.0, 0.0).astype(BF16)

    def groups_of(half):
        return [s + i for s, n in rows_of(half) for i in range(0, n, group)]

    def block_rows(i0, in_half, lanes):
        return jnp.concatenate(
            [a_ref[i0 : i0 + group, s : s + n, lanes] for s, n in rows_of(in_half)], axis=1
        )

    def apply(out_half, in_half, write):
        for n0 in range(0, elements, WIDE):
            lanes = slice(n0, n0 + WIDE)
            right = r_ref[in_half, :, lanes]
            for at, i0 in enumerate(groups_of(out_half)):
                q = (block_rows(i0, in_half, lanes) * right[None]).reshape(depth, WIDE)
                write(slice(at * group, (at + 1) * group), lanes, dot(sum_rows, q))

    def apply_t(out_half, in_half, write):
        for n0 in range(0, elements, WIDE):
            lanes = slice(n0, n0 + WIDE)
            acc = None
            for at, i0 in enumerate(groups_of(in_half)):
                pieces = []
                for i in range(group):
                    row = gf[in_half, at * group + i : at * group + i + 1, lanes]
                    spread = jnp.broadcast_to(row, (BLOCK, WIDE)).astype(BF16)
                    for s, n in rows_of(out_half):
                        pieces.append(a_ref[i0 + i, s : s + n, lanes] * spread)
                now = dot(sum_groups, jnp.concatenate(pieces, axis=0))
                acc = now if acc is None else acc + now
            write(lanes, acc)

    shape = (HALF, elements)

    def rhs(half, u, n, control):
        return (
            u + TIME_STEP * (u - u * u * u)
            + TIME_STEP * PENALTY * (n - faces(half, shape) * u)
            + TIME_STEP * control
        ).astype(BF16)

    loads[0].wait()
    for half in (RIM, MID):
        hist[0, half] = take(st, half)
    x0 = arrange(hist[0, RIM])
    xr[...] = x0
    pl.semaphore_wait(barrier, n_space - 1 + n_tm - 1)
    send_rims(0, x0)
    for c in loads[1:]:
        c.wait()
    for half in (RIM, MID):
        goal[half] = take(tgt, half).astype(F32)

    def forward(k, carry):
        um = hist[k, MID]
        nm = restore(lateral(arrange(um)))
        cm = take(ctl, MID, k).astype(F32)
        cr = take(ctl, RIM, k).astype(F32)
        r_ref[MID] = rhs(MID, um, nm, cm)
        x = xr[...]
        lat = lateral(x)

        @pl.when(k == 0)
        def _():
            for c in a_loads:
                c.wait()

        for out in (RIM, MID):
            def write(rows, lanes, v, out=out):
                hist[k + 1, out, rows, lanes] = v
            apply(out, MID, write)
        ur = hist[k, RIM]
        w = jnp.where(k > 0, weight(k), 0.0)
        dm, dr = um - goal[MID], ur - goal[RIM]
        cost[...] += 0.5 * w * fold(dm * dm + dr * dr) + 0.5 * REGULAR * fold(cm * cm + cr * cr)

        wait_rims(k)
        nr = rim_neighbours(k, x, lat)
        r_ref[RIM] = rhs(RIM, ur, nr, cr)

        def add(out):
            def write(rows, lanes, v):
                hist[k + 1, out, rows, lanes] += v
            return write

        apply(RIM, RIM, add(RIM))

        @pl.when(k < steps - 1)
        def _():
            y = arrange(hist[k + 1, RIM])
            xr[...] = y
            send_rims(k + 1, y)

        apply(MID, RIM, add(MID))
        return carry

    lax.fori_loop(0, steps, forward, 0)

    w_end = weight(steps)
    for half in (MID, RIM):
        u = hist[steps, half]
        d = u - goal[half]
        cost[...] += 0.5 * w_end * fold(d * d)
        gf[half] = w_end * d + take(adj, half)
        st_out[half] = u.astype(BF16)

    def st_copy(dst):
        return pltpu.make_async_remote_copy(
            src_ref=st_out, dst_ref=st_in, send_sem=st_sem.at[0], recv_sem=st_sem.at[1],
            device_id={"tm": dst}, device_id_type=pl.DeviceIdType.MESH)

    @pl.when(t < n_tm - 1)
    def _():
        st_copy(t + 1).start()

    slot_s[me] = cost[...]

    def gather_copy(slots, send, recv, axis, index, count, d):
        return pltpu.make_async_remote_copy(
            src_ref=slots.at[index], dst_ref=slots.at[index], send_sem=send.at[d], recv_sem=recv.at[index],
            device_id={axis: lax.rem(index + d, count)}, device_id_type=pl.DeviceIdType.MESH)

    def gather_wait(slots, send, recv, axis, index, count, d):
        gather_copy(slots, send, recv, axis, index, count, d).wait_send()
        origin = lax.rem(index + d, count)
        pltpu.make_async_remote_copy(
            src_ref=slots.at[origin], dst_ref=slots.at[origin], send_sem=send.at[d], recv_sem=recv.at[origin],
            device_id={axis: origin}, device_id_type=pl.DeviceIdType.MESH).wait_recv()

    over_s = (slot_s, ss_send, ss_recv, "space", me, n_space)
    over_t = (slot_t, tt_send, tt_recv, "tm", t, n_tm)
    for d in range(1, n_space):
        gather_copy(*over_s, d).start()

    def part_write(out):
        def write(lanes, v):
            part[out, :, lanes] = v
        return write

    def pulled_write(out):
        def write(lanes, v):
            pulled[out, :, lanes] = part[out, :, lanes] + v
        return write

    def finish(rnd):
        apply_t(RIM, RIM, pulled_write(RIM))
        y = arrange(pulled[RIM])
        xr[...] = y
        send_rims(rnd, y)
        apply_t(MID, RIM, pulled_write(MID))

    def carry_back(half, k, p, n):
        before = hist[k, half]
        carried = (
            p + TIME_STEP * (1.0 - 3.0 * before * before) * p
            + TIME_STEP * PENALTY * (n - faces(half, shape) * p)
        )
        return before, carried

    def update(half, k, p):
        control = take(ctl, half, k).astype(F32)
        put(newc_ref, half, (control - (TIME_STEP * p + REGULAR * control)).astype(BF16), k)

    apply_t(RIM, MID, part_write(RIM))
    apply_t(MID, MID, part_write(MID))
    finish(steps)

    def backward(i, carry):
        k = steps - 1 - i
        rnd = steps + i
        pm = pulled[MID]
        nm = restore(lateral(arrange(pm)))
        before, carried = carry_back(MID, k, pm, nm)
        gf[MID] = weight(k) * (before - goal[MID]) + carried
        x = xr[...]
        lat = lateral(x)
        apply_t(RIM, MID, part_write(RIM))
        apply_t(MID, MID, part_write(MID))
        pr = pulled[RIM]
        update(MID, k, pm)
        update(RIM, k, pr)

        @pl.when(i == 1)
        def _():
            for d in range(1, n_space):
                gather_wait(*over_s, d)
            total = slot_s[0]
            for j in range(1, n_space):
                total = total + slot_s[j]
            slot_t[t] = total
            for d in range(1, n_tm):
                gather_copy(*over_t, d).start()

        wait_rims(rnd)
        nr = rim_neighbours(rnd, x, lat)
        before_r, carried_r = carry_back(RIM, k, pr, nr)
        gf[RIM] = weight(k) * (before_r - goal[RIM]) + carried_r
        finish(rnd + 1)
        return carry

    lax.fori_loop(0, steps - 1, backward, 0)

    def adj_copy(dst, half):
        return pltpu.make_async_remote_copy(
            src_ref=adj_out.at[half], dst_ref=adj_in.at[half], send_sem=adj_send_sem.at[half],
            recv_sem=adj_recv_sem.at[half], device_id={"tm": dst}, device_id_type=pl.DeviceIdType.MESH)

    def send_adj(half, carried):
        adj_out[half] = carried.astype(adj_out.dtype)

        @pl.when(t > 0)
        def _():
            adj_copy(t - 1, half).start()

    rnd = 2 * steps - 1
    pm, pr = pulled[MID], pulled[RIM]
    nm = restore(lateral(arrange(pm)))
    send_adj(MID, carry_back(MID, 0, pm, nm)[1])
    x = xr[...]
    lat = lateral(x)
    wait_rims(rnd)
    nr = rim_neighbours(rnd, x, lat)
    send_adj(RIM, carry_back(RIM, 0, pr, nr)[1])
    update(MID, 0, pm)
    update(RIM, 0, pr)

    @pl.when(t == 0)
    def _():
        nst_ref[0] = st[...]

    @pl.when(t > 0)
    def _():
        st_copy(t - 1).wait_recv()
        for half in (RIM, MID):
            put(nst_ref, half, st_in[half].astype(F32), 0)

    @pl.when(t < n_tm - 1)
    def _():
        st_copy(t + 1).wait_send()

    for d in range(1, n_tm):
        gather_wait(*over_t, d)
    total = slot_t[0]
    for j in range(1, n_tm):
        total = total + slot_t[j]
    obj_ref[0, 0] = jnp.sum(total) * (1.0 / (total_steps * nodes * elements * n_space))

    @pl.when(t == n_tm - 1)
    def _():
        nadj_ref[...] = jnp.zeros_like(nadj_ref)

    @pl.when(t < n_tm - 1)
    def _():
        for half in (MID, RIM):
            adj_copy(t + 1, half).wait_recv()
            put(nadj_ref, half, adj_in[half].astype(F32), 0)

    @pl.when(t > 0)
    def _():
        for half in (MID, RIM):
            adj_copy(t - 1, half).wait_send()


def store_kernel(count, *refs):
    held = refs[2 * count : 3 * count]
    sems = refs[-1]
    takes = [pltpu.make_async_copy(refs[i], held[i], sems.at[0, i]) for i in range(count)]
    gives = [pltpu.make_async_copy(held[i], refs[count + i], sems.at[1, i]) for i in range(count)]
    for c in takes:
        c.start()
    for take_one, give in zip(takes, gives):
        take_one.wait()
        give.start()
    for c in gives:
        c.wait()


def store(values):
    count = len(values)
    return pl.pallas_call(
        functools.partial(store_kernel, count),
        out_shape=tuple(jax.ShapeDtypeStruct(v.shape, v.dtype) for v in values),
        in_specs=[pl.BlockSpec(memory_space=pltpu.HBM)] * count,
        out_specs=(pl.BlockSpec(memory_space=pltpu.HBM),) * count,
        scratch_shapes=[pltpu.VMEM(v.shape, v.dtype) for v in values] + [pltpu.SemaphoreType.DMA((2, count))],
        compiler_params=pltpu.CompilerParams(vmem_limit_bytes=67043328),
    )(*values)


def solution(mesh):
    n_space, n_tm = mesh.shape["space"], mesh.shape["tm"]

    def per_device(controls, target, state_in, adjoint_in, block_inverse, numbering):
        steps, nodes, elements = controls.shape
        vm = pl.BlockSpec(memory_space=pltpu.VMEM)
        hbm = pl.BlockSpec(memory_space=pltpu.HBM)
        halves = (2, HALF, elements)
        rounds = 2 * steps
        dma = pltpu.SemaphoreType.DMA
        new_controls, next_state, next_adjoint, objective = pl.pallas_call(
            functools.partial(kernel, n_space, n_tm),
            out_shape=(
                jax.ShapeDtypeStruct(controls.shape, BF16),
                jax.ShapeDtypeStruct(state_in.shape, F32),
                jax.ShapeDtypeStruct(adjoint_in.shape, F32),
                jax.ShapeDtypeStruct((1, 1), F32),
            ),
            in_specs=[vm, hbm, hbm, hbm, hbm, hbm],
            out_specs=(vm, vm, vm, pl.BlockSpec(memory_space=pltpu.SMEM)),
            scratch_shapes=[
                pltpu.VMEM(block_inverse.shape, BF16),
                pltpu.VMEM(controls.shape, BF16),
                pltpu.VMEM(target.shape, BF16),
                pltpu.VMEM(adjoint_in.shape[1:], F32),
                pltpu.VMEM(state_in.shape[1:], F32),
                pltpu.VMEM((steps + 1,) + halves, F32),
                pltpu.VMEM(halves, F32),
                pltpu.VMEM(halves, BF16),
                pltpu.VMEM(halves, F32),
                pltpu.VMEM(halves, F32),
                pltpu.VMEM(halves, F32),
                pltpu.VMEM(halves[1:], F32),
                pltpu.VMEM((elements, elements), BF16),
                pltpu.VMEM((elements, elements), BF16),
                pltpu.VMEM((8, 128), F32),
                pltpu.VMEM((rounds, 2, BLOCK, LAYER), BF16),
                pltpu.VMEM((rounds, 2, BLOCK, LAYER), BF16),
                pltpu.VMEM(halves, BF16),
                pltpu.VMEM(halves, BF16),
                pltpu.VMEM(halves, BF16),
                pltpu.VMEM(halves, BF16),
                pltpu.VMEM((n_space, 8, 128), F32),
                pltpu.VMEM((n_tm, 8, 128), F32),
                dma((4,)),
                dma((4,)),
                dma((rounds, 2)),
                dma((rounds, 2)),
                dma((2,)),
                dma((2,)),
                dma((2,)),
                dma((n_space,)),
                dma((n_space,)),
                dma((n_tm,)),
                dma((n_tm,)),
            ],
            compiler_params=pltpu.CompilerParams(
                collective_id=0, has_side_effects=True, vmem_limit_bytes=67043328
            ),
        )(numbering, controls, target, state_in, adjoint_in, block_inverse)
        return store((new_controls, next_state, next_adjoint)) + (objective.reshape(()),)

    return jax.shard_map(
        per_device,
        mesh=mesh,
        in_specs=(
            P("tm", None, "space"),
            P(None, "space"),
            P("tm", None, "space"),
            P("tm", None, "space"),
            P(None, None, "space"),
            P("space", None),
        ),
        out_specs=(P("tm", None, "space"), P("tm", None, "space"), P("tm", None, "space"), P()),
        check_vma=False,
    )
```
